256 devices in a mesh: row: 16 (over x_hi, y, core), col: 16 (over z, x_lo).
Axes of the slice: x: 4 (x_hi: 2, x_lo: 2; x = x_hi * 2 + x_lo), y: 4, z: 8, core: 2. Of those that a mesh axis runs over, the one named last changes fastest.
Arguments:
- train_grads: bfloat16 [8192, 8192], P('row', 'col'), may hold values from -16 to 16
- query_grads: bfloat16 [8192, 8192], P('col', 'row'), may hold values from -6 to 6
Outputs:
- scores: float32 [8192, 8192], P('row', 'col')
The draws below stay inside these ranges and needn't reach their ends.
All inputs are finite; a program needn't handle non-finite values.
Results may differ from the reference program's by a relative error of at most 0.0081.
Values may be sent and summed in bfloat16 or wider, within the bound.
No kernel may reach another device: no remote copies, remote signals or barrier semaphores. Data moves between devices by JAX's collectives and lax.ppermute only.
A program may use at most 128 MiB of HBM per device.

```python
import math
import jax
import jax.numpy as jnp
from jax import lax

PROJ = 64
LAYERS = 2
FEATURES = 8192
TRAIN = 8192
QUERY = 8192


def draw_train_grads(key, part):
    keys = jax.random.split(jax.random.fold_in(key, 71), 5)
    shape = (TRAIN, LAYERS, PROJ, PROJ)
    base = jax.random.truncated_normal(keys[0], -4.0, 4.0, shape, jnp.float32)
    out_scale = jnp.exp(jax.random.uniform(keys[1], (1, LAYERS, PROJ, 1), jnp.float32, 0.0, 2.302585))
    in_scale = jnp.exp(jax.random.uniform(keys[2], (1, LAYERS, 1, PROJ), jnp.float32, 0.0, 2.302585))
    mixing = jnp.eye(PROJ, dtype=jnp.float32) + 0.6 * jax.random.normal(keys[3], (LAYERS, PROJ, PROJ), jnp.float32) / PROJ ** 0.5
    mixed = jnp.einsum('nloi,lij->nloj', base * out_scale, mixing) * in_scale
    ramp = 1.0 + 2.0 * jnp.arange(TRAIN, dtype=jnp.float32) / max(TRAIN - 1, 1)
    jitter = jnp.exp(jax.random.uniform(keys[4], (TRAIN,), jnp.float32, -0.5, 0.5))
    example_scale = (ramp * jitter)[:, None, None, None]
    values = jnp.clip(mixed * example_scale / 30.0, -16.0, 16.0)
    return values.reshape(TRAIN, LAYERS * PROJ * PROJ).astype(jnp.bfloat16)


def steps_of(own_key, dims, cuts, low, high):
    factor_of = 1.0
    for position, shards_of in cuts:
        steps = jax.random.uniform(jax.random.fold_in(jax.random.fold_in(own_key, 6), position), (shards_of,), jnp.float32, low / len(cuts), high / len(cuts))
        factor_of = factor_of * jnp.repeat(jnp.exp(steps), dims[position] // shards_of).reshape((-1,) + (1,) * (len(dims) - 1 - position))
    return factor_of


def noise(key, shape, width, limit, cuts=(), held_as=jnp.bfloat16):
    factor_of = steps_of(key, shape, cuts, -0.22, 0.18) if cuts else 1.0
    drawn = jax.random.normal(key, shape, jnp.float32) * width * factor_of
    return jnp.minimum(jnp.maximum(drawn, -limit), limit).astype(held_as)


def setup_inputs(seed: int = 0) -> dict:
    key_of = jax.random.split(jax.random.key(seed), 3)
    train_grads = draw_train_grads(jax.random.fold_in(key_of[2], 71), 0)
    query_grads = noise(key_of[1], (QUERY, FEATURES), 1.0, 6.0, ((0, 16), (1, 16)))
    return {"train_grads": train_grads, "query_grads": query_grads}


damping_ratio = 0.1

def invert_factors(factors):
    size = factors.shape[-1]
    identity = jnp.eye(size, dtype=jnp.float32)
    trace_value = jnp.trace(factors, axis1=1, axis2=2)
    damped = factors + damping_ratio * (trace_value / size)[:, None, None] * identity
    lower_factor = lax.linalg.cholesky(damped)
    lower_inverse = lax.linalg.triangular_solve(lower_factor, jnp.broadcast_to(identity, damped.shape), left_side=True, lower=True)
    result = jnp.einsum('kji,kjl->kil', lower_inverse, lower_inverse, precision=lax.Precision.HIGHEST)
    return result.astype(jnp.bfloat16)

def precondition(queries, inverses):
    layer_count = inverses.shape[0] // 2
    size = inverses.shape[-1]
    count_rows = queries.shape[0]
    values = queries.astype(jnp.float32).reshape(count_rows, layer_count, size, size)
    input_inverse = inverses[:layer_count].astype(jnp.float32)
    output_inverse = inverses[layer_count:].astype(jnp.float32)
    half = jnp.einsum('nloi,lij->nloj', values, input_inverse, precision=lax.Precision.HIGHEST).astype(jnp.bfloat16)
    result = jnp.einsum('lop,nlpj->nloj', output_inverse, half.astype(jnp.float32), precision=lax.Precision.HIGHEST)
    return result.reshape(count_rows, -1).astype(jnp.bfloat16)

def reference(train_grads, query_grads):
    grads = train_grads.astype(jnp.float32).reshape(TRAIN, LAYERS, PROJ, PROJ)
    input_factor = jnp.einsum('nloi,nloj->lij', grads, grads, precision=lax.Precision.HIGHEST)
    output_factor = jnp.einsum('nloi,nlpi->lop', grads, grads, precision=lax.Precision.HIGHEST)
    factors = jnp.concatenate([input_factor, output_factor], axis=0) / (TRAIN * PROJ)
    inverses = invert_factors(factors)
    conditioned = precondition(query_grads, inverses)
    total = jnp.dot(train_grads.astype(jnp.float32), conditioned.T.astype(jnp.float32), preferred_element_type=jnp.float32)
    return total * (1.0 / math.sqrt(LAYERS * PROJ * PROJ))
```

```python
import math

import jax
import jax.numpy as jnp
from jax import lax
from jax.experimental import pallas as pl
from jax.experimental.pallas import tpu as pltpu
from jax.sharding import Mesh
from jax.sharding import PartitionSpec as P

PROJ = 64
LAYERS = 2
ROW = ("xh", "y", "co")
COL = ("zh", "zl", "xl")
Z = ("zh", "zl")
DAMPING = 0.1
SWAP = [(0, 1), (1, 0)]
F32 = jnp.float32
BF16 = jnp.bfloat16
VMEM = pl.BlockSpec(memory_space=pltpu.VMEM)
SMEM = pl.BlockSpec(memory_space=pltpu.SMEM)


def shift(value, axis, size, step):
    return lax.ppermute(value, axis, [(i, (i + step) % size) for i in range(size)])


def swap(value, axis):
    return lax.ppermute(value, axis, SWAP)


def iota(shape, dim):
    return lax.broadcasted_iota(jnp.int32, shape, dim)


def inverse_kernel(count, factor_ref, wide_in_ref, wide_out_ref):
    factors = factor_ref[...] * (1.0 / count)
    shape = factors.shape
    rows, cols = iota(shape, 1), iota(shape, 2)
    trace = jnp.sum(
        jnp.sum(jnp.where(rows == cols, factors, 0.0), axis=2, keepdims=True), axis=1, keepdims=True
    )
    damped = factors + jnp.where(rows == cols, DAMPING * (trace / PROJ), 0.0)

    def step(k, a):
        on_col, on_row = cols == k, rows == k
        col = jnp.sum(jnp.where(on_col, a, 0.0), axis=2, keepdims=True)
        row = jnp.sum(jnp.where(on_row, a, 0.0), axis=1, keepdims=True)
        row_on = iota(row.shape, 2) == k
        pivot = jnp.sum(jnp.where(row_on, row, 0.0), axis=2, keepdims=True)
        scale = 1.0 / pivot
        row = jnp.where(row_on, scale, row * scale)
        return jnp.where(on_row, row, jnp.where(on_col, 0.0, a) - col * row)

    inverse = lax.fori_loop(0, PROJ, step, damped).astype(BF16)

    r, i = iota((256, PROJ), 0), iota((256, PROJ), 1)
    pick_in = (i == (r // 32) * 8 + r % 8).astype(BF16)
    j, c = iota((PROJ, 256), 0), iota((PROJ, 256), 1)
    spread_in = (c % PROJ == j).astype(BF16)
    r, c = iota((256, 256), 0), iota((256, 256), 1)
    keep_in = (r // 8) % 4 == c // PROJ
    r, o = iota((512, PROJ), 0), iota((512, PROJ), 1)
    pick_out = (o == r // 8).astype(BF16)
    o, c = iota((PROJ, 512), 0), iota((PROJ, 512), 1)
    spread_out = (o == c // 8).astype(BF16)
    r, c = iota((512, 512), 0), iota((512, 512), 1)
    keep_out = r % 8 == c % 8
    for layer in range(LAYERS):
        part = jnp.dot(pick_in, inverse[layer], preferred_element_type=F32).astype(BF16)
        part = jnp.dot(part, spread_in, preferred_element_type=F32)
        wide_in_ref[layer] = jnp.where(keep_in, part, 0.0).astype(BF16)
        part = jnp.dot(pick_out, inverse[LAYERS + layer], preferred_element_type=F32).astype(BF16)
        part = jnp.dot(part, spread_out, preferred_element_type=F32)
        wide_out_ref[layer] = jnp.where(keep_out, part, 0.0).astype(BF16)


def inverses(factors, count):
    return pl.pallas_call(
        lambda *refs: inverse_kernel(count, *refs),
        out_shape=(
            jax.ShapeDtypeStruct((LAYERS, 256, 256), BF16),
            jax.ShapeDtypeStruct((LAYERS, 512, 512), BF16),
        ),
        in_specs=[VMEM],
        out_specs=(VMEM, VMEM),
        name="inverses",
    )(factors)


def condition_kernel(places, where_ref, wide_in_ref, wide_out_ref, *refs):
    pieces, out_ref, half_ref = refs[: len(places)], refs[-2], refs[-1]
    me = where_ref[0]
    xh, y, co = me // 8, (me // 2) % 4, me % 2
    for ref, spots in zip(pieces, places):
        for first, dxh, dy, dco in spots:
            layer = jnp.bitwise_xor(xh, dxh)
            block = ((y + dy) % 4) * 2 + jnp.bitwise_xor(co, dco)
            for part in range(2):
                half = jnp.dot(
                    wide_in_ref[layer],
                    ref[first + part * 256 : first + (part + 1) * 256, :],
                    preferred_element_type=F32,
                ).astype(BF16)
                start = pl.multiple_of((block * 2 + part) * 32, 32)
                half_ref[layer, :, pl.ds(start, 32), :] = half.reshape(8, 32, half.shape[-1])
    for layer in range(LAYERS):

        @pl.loop(0, 4)
        def _(k):
            both = [
                jnp.dot(wide_out_ref[layer], half_ref[layer, 2 * k + g], preferred_element_type=F32)
                .reshape(PROJ, 8, half_ref.shape[-1])
                for g in range(2)
            ]
            start = pl.multiple_of(16 * k, 16)
            out_ref[layer, :, pl.ds(start, 16), :] = jnp.concatenate(both, axis=1).astype(BF16)


def condition(where, wide_in, wide_out, pieces, places):
    queries = pieces[0].shape[-1]
    shape = (LAYERS, PROJ, PROJ, queries)
    return pl.pallas_call(
        lambda *refs: condition_kernel(places, *refs),
        out_shape=jax.ShapeDtypeStruct(shape, BF16),
        in_specs=[SMEM] + [VMEM] * (2 + len(pieces)),
        out_specs=VMEM,
        scratch_shapes=[pltpu.VMEM((LAYERS, 8, 512, queries), BF16)],
        name="condition",
    )(where, wide_in, wide_out, *pieces)


def score_kernel(places, scale, where_ref, cond_ref, *refs):
    pieces, out_ref = refs[: len(places)], refs[-1]
    me = where_ref[0]
    z, a = me // 2, me % 2
    out_ref[...] = jnp.zeros_like(out_ref)
    for ref, spots in zip(pieces, places):
        for first, count, row, dz, other in spots:
            slot = ((z + dz) % 8) * 2 + jnp.bitwise_xor(a, other)
            start = pl.multiple_of(slot * 512, 512)
            out_ref[row : row + count, :] += jnp.dot(
                ref[first : first + count, :], cond_ref[pl.ds(start, 512), :], preferred_element_type=F32
            )
    out_ref[...] = out_ref[...] * scale


def score(where, cond, pieces, places, rows, scale):
    return pl.pallas_call(
        lambda *refs: score_kernel(places, scale, *refs),
        out_shape=jax.ShapeDtypeStruct((rows, cond.shape[-1]), F32),
        in_specs=[SMEM] + [VMEM] * (1 + len(pieces)),
        out_specs=VMEM,
        name="score",
    )(where, cond, *pieces)


def all_of(value, axis, size):
    total = value
    for k in range(1, size):
        total = total + lax.ppermute(value, axis, [(i, i ^ k) for i in range(size)])
    return total


def local(train, query):
    bar = lax.optimization_barrier
    rows = train.shape[0]
    low = rows // 2
    features = train.shape[1] * 16
    ex = lax.all_to_all(train.reshape(8, rows // 8, 512), ("zl", "xl"), 0, 0, tiled=True)

    qt = query.T
    qx = swap(qt, "xh")
    q0 = jnp.concatenate([qt, qx], axis=0)
    partner = swap(train[low:], "xl")

    blocks = ex.reshape(8, rows // 8, 8, PROJ)
    out_side = jnp.einsum("anoi,bnpi->aobp", blocks, blocks, preferred_element_type=F32)
    in_side = jnp.einsum("anoi,anoj->ij", blocks, blocks, preferred_element_type=F32)
    total = jnp.stack([in_side, out_side.reshape(PROJ, PROJ)])
    total = all_of(total, "co", 2)
    total = all_of(total, ("xh", "xl"), 4)
    total = all_of(total, "y", 4)
    total = all_of(total, "zl", 4)
    other = swap(total, "zh")
    first = lax.axis_index("zh") == 0
    layer0 = jnp.where(first, total, other)
    layer1 = jnp.where(first, other, total)
    factors = jnp.stack([layer0[0], layer1[0], layer0[1], layer1[1]])
    count = rows * 16 * PROJ
    wide_in, wide_out = inverses(factors, count)

    qm = shift(q0, "y", 4, 1)
    qp = shift(q0, "y", 4, -1)
    q2a = shift(qm[:512], "y", 4, 1)
    q2b = shift(qp[512:], "y", 4, -1)
    groups = [
        (q0, [(0, 0, 0), (512, 1, 0)]),
        (qm, [(0, 0, 3), (512, 1, 3)]),
        (qp, [(0, 0, 1), (512, 1, 1)]),
        (q2a, [(0, 0, 2)]),
        (q2b, [(0, 1, 2)]),
    ]
    pieces, places = [], []
    for dco in range(2):
        for value, spots in groups:
            pieces.append(value if dco == 0 else swap(value, "co"))
            places.append([(f, dxh, dy, dco) for f, dxh, dy in spots])
    me_row = lax.axis_index(ROW).astype(jnp.int32).reshape(1)
    cond = condition(me_row, wide_in, wide_out, pieces, places)
    cond = cond.reshape(features, cond.shape[-1])

    held = jnp.concatenate([train, partner], axis=0)
    held, _ = bar((held, ex))
    pieces, places = [train, partner], [[(0, rows, 0, 0, 0)], [(0, low, low, 0, 1)]]
    down, up = held, held
    tops = [train[:low]]
    for k in range(1, 4):
        down, up = shift(down, Z, 8, 1), shift(up, Z, 8, -1)
        for value, dz in ((down, 8 - k), (up, k)):
            pieces.append(value)
            places.append([(0, rows, 0, dz, 0), (rows, low, low, dz, 1)])
        tops.append(jnp.concatenate([down[:low], up[:low]], axis=0))
    cut = (rows + low) // 2
    far_a = shift(down[:cut], Z, 8, 1)
    far_b = shift(up[cut:], Z, 8, -1)
    pieces += [far_a, far_b]
    places += [[(0, cut, 0, 4, 0)], [(0, rows - cut, cut, 4, 0), (rows - cut, low, low, 4, 1)]]
    tops.append(far_a[:low])
    for k, top in enumerate(tops):
        pieces.append(swap(top, "xl"))
        if k in (0, 4):
            places.append([(0, low, 0, k, 1)])
        else:
            places.append([(0, low, 0, 8 - k, 1), (low, low, 0, k, 1)])
    me_col = lax.axis_index(COL).astype(jnp.int32).reshape(1)
    return score(me_col, cond, pieces, places, rows, 1.0 / math.sqrt(features))


def solution(mesh):
    torus = Mesh(mesh.devices.reshape(2, 4, 2, 2, 4, 2), ROW + COL)
    in_specs = (P(ROW, COL), P(COL, ROW))
    return jax.shard_map(local, mesh=torus, in_specs=in_specs, out_specs=P(ROW, COL), check_vma=False)
```

```python
import math

import jax
import jax.numpy as jnp
from jax import lax
from jax.experimental import pallas as pl
from jax.experimental.pallas import tpu as pltpu
from jax.sharding import Mesh
from jax.sharding import PartitionSpec as P


PROJ = 64
LAYERS = 2
ROW = ("xh", "y", "co")
COL = ("zh", "zl", "xl")
Z = ("zh", "zl")
DAMPING = 0.1
SWAP = [(0, 1), (1, 0)]
F32 = jnp.float32
BF16 = jnp.bfloat16
VMEM = pl.BlockSpec(memory_space=pltpu.VMEM)
SMEM = pl.BlockSpec(memory_space=pltpu.SMEM)
ANY = pl.BlockSpec(memory_space=pl.ANY)
HBM = pl.BlockSpec(memory_space=pltpu.HBM)


def ring(value, axes, size):
    pairs = []
    for core, step in ((0, 1), (1, -1)):
        for n in range(size):
            to = (n + step) % size
            pair = (core * size + n, core * size + to) if axes[0] == "co" else (2 * n + core, 2 * to + core)
            pairs.append(pair)
    return lax.ppermute(value, axes, pairs)


def swap(value, axis):
    return lax.ppermute(value, axis, SWAP)


def iota(shape, dim):
    return lax.broadcasted_iota(jnp.int32, shape, dim)


def invert(mats):
    shape = (PROJ, PROJ)
    rows, cols, lane = iota(shape, 0), iota(shape, 1), iota((1, PROJ), 1)

    def at(mask, value, axis=1):
        return jnp.sum(jnp.where(mask, value, 0.0), axis=axis, keepdims=True)

    def step(t, mats):
        k = 2 * t
        col0, col1, row0, row1 = cols == k, cols == k + 1, rows == k, rows == k + 1
        lane0, lane1 = lane == k, lane == k + 1
        out = []
        for a in mats:
            c0, c1 = at(col0, a), at(col1, a)
            r0, r1 = at(row0, a, 0), at(row1, a, 0)
            p, q, u, v = at(lane0, r0), at(lane1, r0), at(lane0, r1), at(lane1, r1)
            d = 1.0 / (p * v - q * u)
            r0 = jnp.where(lane0, 1.0, jnp.where(lane1, 0.0, r0))
            r1 = jnp.where(lane1, 1.0, jnp.where(lane0, 0.0, r1))
            n0 = (v * d) * r0 - (q * d) * r1
            n1 = (p * d) * r1 - (u * d) * r0
            rest = jnp.where(col0 | col1, 0.0, a) - c0 * n0 - c1 * n1
            out.append(jnp.where(row0, n0, jnp.where(row1, n1, rest)))
        return tuple(out)

    return lax.fori_loop(0, PROJ // 2, step, tuple(mats))


def inverse_kernel(count, factor_ref, out_ref):
    rows, cols = iota((PROJ, PROJ), 0), iota((PROJ, PROJ), 1)
    mats = []
    for n in range(2):
        factor = factor_ref[n] * (1.0 / count)
        diagonal = jnp.where(rows == cols, factor, 0.0)
        trace = jnp.sum(jnp.sum(diagonal, axis=1, keepdims=True), axis=0, keepdims=True)
        mats.append(factor + jnp.where(rows == cols, DAMPING * (trace / PROJ), 0.0))
    for n, inverse in enumerate(invert(mats)):
        out_ref[n] = inverse.astype(BF16)


def inverses(factors, count):
    return pl.pallas_call(
        lambda *refs: inverse_kernel(count, *refs),
        out_shape=jax.ShapeDtypeStruct((2, PROJ, PROJ), BF16),
        in_specs=[VMEM],
        out_specs=VMEM,
        compiler_params=pltpu.CompilerParams(vmem_limit_bytes=8 << 20),
        cost_estimate=pl.CostEstimate(flops=10**8, bytes_accessed=1 << 20, transcendentals=0),
        name="inverses",
    )(factors)


def expand(inverse_ref, wide_in_ref, wide_out_ref):
    r, i = iota((256, PROJ), 0), iota((256, PROJ), 1)
    pick_in = (i == (r // 32) * 8 + r % 8).astype(BF16)
    j, c = iota((PROJ, 256), 0), iota((PROJ, 256), 1)
    spread_in = (c % PROJ == j).astype(BF16)
    r, c = iota((256, 256), 0), iota((256, 256), 1)
    part = jnp.dot(pick_in, inverse_ref[0], preferred_element_type=F32).astype(BF16)
    part = jnp.dot(part, spread_in, preferred_element_type=F32)
    wide_in_ref[...] = jnp.where((r // 8) % 4 == c // PROJ, part, 0.0).astype(BF16)
    r, o = iota((512, PROJ), 0), iota((512, PROJ), 1)
    pick_out = (o == r // 8).astype(BF16)
    o, c = iota((PROJ, 512), 0), iota((PROJ, 512), 1)
    spread_out = (o == c // 8).astype(BF16)
    r, c = iota((512, 512), 0), iota((512, 512), 1)
    part = jnp.dot(pick_out, inverse_ref[1], preferred_element_type=F32).astype(BF16)
    part = jnp.dot(part, spread_out, preferred_element_type=F32)
    wide_out_ref[...] = jnp.where(r % 8 == c % 8, part, 0.0).astype(BF16)


def fetch_queries(near, far, use_near, query_buf, query_sem):
    copies = [
        [pltpu.make_async_copy(r, query_buf.at[n], query_sem.at[n]) for n, r in enumerate(refs)]
        for refs in (near, far)
    ]

    @pl.when(use_near)
    def _():
        start_all(copies[0])

    @pl.when(jnp.logical_not(use_near))
    def _():
        start_all(copies[1])

    return copies[0]


def condition_layer(places, me, copies, query_buf, half_ref, wide_in_ref, wide_out_ref, store):
    y, co = (me // 2) % 4, me % 2
    toward = 2 * co - 1
    width = half_ref.shape[-1]
    for n, (dy, along, dco) in enumerate(places):
        copies[n].wait()
        block = ((y + dy + along * toward + 4) % 4) * 2 + jnp.bitwise_xor(co, dco)
        for part in range(2):
            half = jnp.dot(
                wide_in_ref[...],
                query_buf[n, part * 256 : (part + 1) * 256, :],
                preferred_element_type=F32,
            ).astype(BF16)
            start = pl.multiple_of((block * 2 + part) * 32, 32)
            half_ref[:, pl.ds(start, 32), :] = half.reshape(8, 32, width)

    @pl.loop(0, 4)
    def _(k):
        both = [
            jnp.dot(wide_out_ref[...], half_ref[2 * k + g], preferred_element_type=F32)
            .reshape(PROJ, 8, width)
            for g in range(2)
        ]
        store(k, pl.multiple_of(16 * k, 16), jnp.concatenate(both, axis=1).astype(BF16))


def first_kernel(places, me_row_ref, me_col_ref, inverse_ref, *refs):
    near, far = refs[:8], refs[8:16]
    out_ref, query_buf, half_ref, cond_ref, wide_in_ref, wide_out_ref, query_sem, out_sem = refs[16:]
    me = me_row_ref[0]
    layer = (me_col_ref[0] // 8) % 2
    copies = fetch_queries(near, far, me // 8 == layer, query_buf, query_sem)
    expand(inverse_ref, wide_in_ref, wide_out_ref)

    def out_copy(k, start):
        rows = pl.ds(start, 16)
        return pltpu.make_async_copy(cond_ref.at[:, rows, :], out_ref.at[:, rows, :], out_sem.at[k])

    def store(k, start, value):
        cond_ref[:, pl.ds(start, 16), :] = value
        out_copy(k, start).start()

    condition_layer(places, me, copies, query_buf, half_ref, wide_in_ref, wide_out_ref, store)
    for k in range(4):
        out_copy(k, 16 * k).wait()


def condition_first(me_row, me_col, inverse, near, far, places):
    width = near[0].shape[-1]
    return pl.pallas_call(
        lambda *refs: first_kernel(places, *refs),
        out_shape=jax.ShapeDtypeStruct((PROJ, PROJ, width), BF16),
        in_specs=[SMEM, SMEM, VMEM] + [ANY] * 16,
        out_specs=HBM,
        scratch_shapes=[
            pltpu.VMEM((8, 512, width), BF16),
            pltpu.VMEM((8, 512, width), BF16),
            pltpu.VMEM((PROJ, PROJ, width), BF16),
            pltpu.VMEM((256, 256), BF16),
            pltpu.VMEM((512, 512), BF16),
            pltpu.SemaphoreType.DMA((8,)),
            pltpu.SemaphoreType.DMA((4,)),
        ],
        compiler_params=pltpu.CompilerParams(vmem_limit_bytes=20 << 20),
        cost_estimate=pl.CostEstimate(flops=3 * 10**9, bytes_accessed=8 << 20, transcendentals=0),
        name="condition_first",
    )(me_row, me_col, inverse, *near, *far)


def input_kernel(x_ref, out_ref):
    x = x_ref[...]
    gram = lax.dot_general(x, x, (((0,), (0,)), ((), ())), preferred_element_type=F32)
    gram = jnp.where(iota(gram.shape, 0) // PROJ == iota(gram.shape, 1) // PROJ, gram, 0.0)
    rows = jnp.sum(gram.reshape(8, PROJ, 512), axis=0)
    fold = rows[:, :128] + rows[:, 128:256] + rows[:, 256:384] + rows[:, 384:]
    out_ref[...] = fold[:, :PROJ] + fold[:, PROJ:]


def input_factor(train):
    return pl.pallas_call(
        input_kernel,
        out_shape=jax.ShapeDtypeStruct((PROJ, PROJ), F32),
        in_specs=[VMEM],
        out_specs=VMEM,
        compiler_params=pltpu.CompilerParams(vmem_limit_bytes=8 << 20),
        cost_estimate=pl.CostEstimate(flops=3 * 10**8, bytes_accessed=1 << 20, transcendentals=0),
        name="input_factor",
    )(train)


def terms_kernel(x_ref, input_ref, out_ref, side_ref, sum_ref):
    blocks, count, _ = x_ref.shape
    for b in range(blocks):
        turned = x_ref[b].astype(F32).T.astype(BF16).reshape(8, 4, 16, count)
        parts = [turned[:, g].reshape(128, count) for g in range(4)]
        side_ref[b * 128 : (b + 1) * 128, :] = jnp.concatenate(parts, axis=1)
    for b in range(blocks):
        gram = lax.dot_general(
            side_ref[b * 128 : (b + 1) * 128, :],
            side_ref[...],
            (((1,), (1,)), ((), ())),
            preferred_element_type=F32,
        )
        gram = jnp.where(iota(gram.shape, 0) % 16 == iota(gram.shape, 1) % 16, gram, 0.0)
        sum_ref[8 * b : 8 * b + 8, :] = jnp.sum(gram.reshape(8, 16, 1024), axis=1)
    ones = (iota((1024, PROJ), 0) // 16 == iota((1024, PROJ), 1)).astype(BF16)
    rest = sum_ref[...]
    total = jnp.zeros((PROJ, PROJ), F32)
    for _ in range(3):
        part = rest.astype(BF16)
        total += jnp.dot(part, ones, preferred_element_type=F32)
        rest = rest - part.astype(F32)
    out_ref[0] = input_ref[...]
    out_ref[1] = total


def factor_terms(blocks, input_term):
    count = blocks.shape[1]
    return pl.pallas_call(
        terms_kernel,
        out_shape=jax.ShapeDtypeStruct((2, PROJ, PROJ), F32),
        in_specs=[VMEM, VMEM],
        out_specs=VMEM,
        scratch_shapes=[pltpu.VMEM((1024, 4 * count), BF16), pltpu.VMEM((PROJ, 1024), F32)],
        compiler_params=pltpu.CompilerParams(vmem_limit_bytes=12 << 20),
        cost_estimate=pl.CostEstimate(flops=6 * 10**8, bytes_accessed=1 << 20, transcendentals=0),
        name="factor_terms",
    )(blocks, input_term)


def column_of(me, k, other):
    toward = jnp.where((me // 16) % 2 == 0, -k, k)
    return ((me // 2 + toward) % 8) * 2 + jnp.bitwise_xor(me % 2, other)


def start_all(copies):
    for copy in copies:
        copy.start()
    return copies


def main_kernel(places, own_places, me_row_ref, me_col_ref, inverse_ref, first_ref, *refs):
    near, far, theirs_refs, refs = refs[:8], refs[8:16], refs[16:22], refs[22:]
    own_refs, refs = refs[: len(own_places)], refs[len(own_places) :]
    out_ref, own_ref, late_ref, query_buf, half_ref, cond_ref, sum_ref, wide_in_ref, wide_out_ref = refs[:9]
    theirs_buf, own_buf, query_sem, theirs_sem, own_sem, late_sem, first_sem = refs[9:]

    me = me_row_ref[0]
    layer = (me_col_ref[0] // 8) % 2
    query_copies = fetch_queries(near, far, me // 8 != layer, query_buf, query_sem)
    first_start = pl.multiple_of(layer * PROJ, PROJ)
    first_copy = pltpu.make_async_copy(first_ref, cond_ref.at[pl.ds(first_start, PROJ)], first_sem.at[0])
    first_copy.start()
    theirs_copies = start_all(
        [pltpu.make_async_copy(r, theirs_buf.at[n], theirs_sem.at[n]) for n, r in enumerate(theirs_refs)]
    )
    own_copies = start_all(
        [
            pltpu.make_async_copy(r, own_buf.at[pl.ds(first * 512, slots * 512)], own_sem.at[first])
            for r, (first, slots) in zip(own_refs, own_places)
        ]
    )
    expand(inverse_ref, wide_in_ref, wide_out_ref)
    width = half_ref.shape[-1]
    second_start = pl.multiple_of((1 - layer) * PROJ, PROJ)

    def store(k, start, value):
        cond_ref[pl.ds(second_start, PROJ), pl.ds(start, 16), :] = value

    condition_layer(places, me, query_copies, query_buf, half_ref, wide_in_ref, wide_out_ref, store)
    first_copy.wait()

    me = me_col_ref[0]
    late_copies = start_all(
        [
            pltpu.make_async_copy(
                cond_ref.at[pl.ds(column_of(me, 3 + n // 2, n % 2) * 8, 8)], late_ref.at[n], late_sem.at[n]
            )
            for n in range(4)
        ]
    )

    def cond_of(k, other):
        return cond_ref[pl.ds(column_of(me, k, other) * 8, 8)].reshape(512, width)

    for n in range(6):
        theirs_copies[n].wait()
        part = jnp.dot(theirs_buf[n], cond_of(1 + n // 2, n % 2), preferred_element_type=F32)
        sum_ref[...] = part if n == 0 else sum_ref[...] + part
    out_ref[...] = sum_ref[...].astype(BF16)
    waits = {first: copy for copy, (first, _) in zip(own_copies, own_places)}
    for n in range(6):
        if n in waits:
            waits[n].wait()
        part = jnp.dot(
            own_buf[n * 512 : (n + 1) * 512, :], cond_of(n // 2, n % 2), preferred_element_type=F32
        )
        own_ref[...] = part if n == 0 else own_ref[...] + part
    for copy in late_copies:
        copy.wait()


def condition_and_score(me_row, me_col, inverse, first, near, far, places, theirs, own, own_places):
    width = near[0].shape[-1]
    return pl.pallas_call(
        lambda *refs: main_kernel(places, own_places, *refs),
        out_shape=(
            jax.ShapeDtypeStruct((512, width), BF16),
            jax.ShapeDtypeStruct((512, width), F32),
            jax.ShapeDtypeStruct((4, 8, PROJ, width), BF16),
        ),
        in_specs=[SMEM, SMEM, VMEM, HBM] + [ANY] * (16 + len(theirs) + len(own)),
        out_specs=(VMEM, VMEM, HBM),
        scratch_shapes=[
            pltpu.VMEM((8, 512, width), BF16),
            pltpu.VMEM((8, 512, width), BF16),
            pltpu.VMEM((LAYERS * PROJ, PROJ, width), BF16),
            pltpu.VMEM((512, width), F32),
            pltpu.VMEM((256, 256), BF16),
            pltpu.VMEM((512, 512), BF16),
            pltpu.VMEM((6, 512, 512), BF16),
            pltpu.VMEM((6 * 512, 512), BF16),
            pltpu.SemaphoreType.DMA((8,)),
            pltpu.SemaphoreType.DMA((6,)),
            pltpu.SemaphoreType.DMA((6,)),
            pltpu.SemaphoreType.DMA((4,)),
            pltpu.SemaphoreType.DMA((1,)),
        ],
        compiler_params=pltpu.CompilerParams(vmem_limit_bytes=34 << 20),
        cost_estimate=pl.CostEstimate(flops=6 * 10**9, bytes_accessed=18 << 20, transcendentals=0),
        name="condition_and_score",
    )(me_row, me_col, inverse, first, *near, *far, *theirs, *own)


def own_kernel(total_ref, cond_ref, near_ref, far_ref, out_ref):
    total = total_ref[...]
    for n in range(4):
        ref = (near_ref, far_ref)[n // 2]
        rows = ref[n % 2 * 512 : (n % 2 + 1) * 512, :]
        total += jnp.dot(
            rows, cond_ref[n].reshape(512, cond_ref.shape[-1]), preferred_element_type=F32
        )
    out_ref[...] = total


def score_own(total, cond, near, far):
    return pl.pallas_call(
        own_kernel,
        out_shape=jax.ShapeDtypeStruct(total.shape, F32),
        in_specs=[VMEM] * 4,
        out_specs=VMEM,
        compiler_params=pltpu.CompilerParams(vmem_limit_bytes=12 << 20),
        cost_estimate=pl.CostEstimate(flops=10**9, bytes_accessed=5 << 20, transcendentals=0),
        name="score_own",
    )(total, cond, near, far)


def all_of(value, axis, size):
    total = value
    for k in range(1, size):
        total = total + lax.ppermute(value, axis, [(i, i ^ k) for i in range(size)])
    return total


def local(train, query):
    rows = train.shape[0]
    features = train.shape[1] * 16
    partner = swap(train, "xl")
    ex = lax.all_to_all(train.reshape(8, rows // 8, 512), ("zl", "xl"), 0, 0, tiled=True)
    total = factor_terms(ex, input_factor(train))
    total = all_of(total, "co", 2)
    total = all_of(total, "y", 4)
    total = all_of(total, ("xh", "xl"), 4)
    total = all_of(total, "zl", 4)
    inverse = inverses(total, rows * 16 * PROJ)
    other_inverse = swap(inverse, "zh")

    queries = []
    for tag in "qx":
        value = query.T if tag == "q" else swap(value, "xh")
        other = swap(value, "co")
        next_own = ring(value, ("y", "co"), 4)
        next_other = ring(other, ("y", "co"), 4)
        far_own = ring(next_own, ("y", "co"), 4)
        queries.append(
            [
                value,
                other,
                next_own,
                next_other,
                swap(next_own, "co"),
                swap(next_other, "co"),
                far_own,
                swap(far_own, "co"),
            ]
        )
    places = ((0, 0, 0), (0, 0, 1), (0, 1, 0), (0, 1, 1), (0, -1, 1), (0, -1, 0), (2, 0, 0), (2, 0, 1))

    a = jnp.concatenate([train, partner], axis=0)
    b = swap(train, "co")
    ring_axes = ("co",) + Z
    mine, others = [train, partner], []
    for k in range(1, 5):
        a = ring(a, ring_axes, 8)
        mine.append(a)
        if k < 4:
            b = ring(b, ring_axes, 8)
            others += [b, swap(b, "xl")]
    me_row = lax.axis_index(ROW).astype(jnp.int32).reshape(1)
    me_col = lax.axis_index(("co",) + COL).astype(jnp.int32).reshape(1)
    own_places = ((0, 1), (1, 1), (2, 2), (4, 2))
    first = condition_first(me_row, me_col, inverse, *queries, places)
    theirs, own, cond = condition_and_score(
        me_row, me_col, other_inverse, first, *queries, places, others, mine[:4], own_places
    )
    theirs = swap(theirs, "co").astype(F32)
    return (score_own(own, cond, *mine[4:]) + theirs) * (1.0 / math.sqrt(features))


def solution(mesh):
    torus = Mesh(mesh.devices.reshape(2, 4, 2, 2, 4, 2), ROW + COL)
    in_specs = (P(ROW, COL), P(COL, ROW))
    return jax.shard_map(local, mesh=torus, in_specs=in_specs, out_specs=P(ROW, COL), check_vma=False)
```

```python
import math

import jax
import jax.numpy as jnp
from jax import lax
from jax.experimental import pallas as pl
from jax.experimental.pallas import tpu as pltpu
from jax.sharding import Mesh
from jax.sharding import PartitionSpec as P


PROJ = 64
LAYERS = 2
ROW = ("xh", "y", "co")
COL = ("zh", "zl", "xl")
Z = ("zh", "zl")
DAMPING = 0.1
SWAP = [(0, 1), (1, 0)]
F32 = jnp.float32
BF16 = jnp.bfloat16
VMEM = pl.BlockSpec(memory_space=pltpu.VMEM)
SMEM = pl.BlockSpec(memory_space=pltpu.SMEM)
ANY = pl.BlockSpec(memory_space=pl.ANY)
HBM = pl.BlockSpec(memory_space=pltpu.HBM)


def ring(value, axes, size):
    pairs = []
    for core, step in ((0, 1), (1, -1)):
        for n in range(size):
            to = (n + step) % size
            pair = (core * size + n, core * size + to) if axes[0] == "co" else (2 * n + core, 2 * to + core)
            pairs.append(pair)
    return lax.ppermute(value, axes, pairs)


def swap(value, axis):
    return lax.ppermute(value, axis, SWAP)


def iota(shape, dim):
    return lax.broadcasted_iota(jnp.int32, shape, dim)


def invert(mats):
    shape = (PROJ, PROJ)
    rows, cols, lane = iota(shape, 0), iota(shape, 1), iota((1, PROJ), 1)

    def at(mask, value, axis=1):
        return jnp.sum(jnp.where(mask, value, 0.0), axis=axis, keepdims=True)

    def step(t, mats):
        k = 2 * t
        col0, col1, row0, row1 = cols == k, cols == k + 1, rows == k, rows == k + 1
        lane0, lane1 = lane == k, lane == k + 1
        out = []
        for a in mats:
            c0, c1 = at(col0, a), at(col1, a)
            r0, r1 = at(row0, a, 0), at(row1, a, 0)
            p, q, u, v = at(lane0, r0), at(lane1, r0), at(lane0, r1), at(lane1, r1)
            d = 1.0 / (p * v - q * u)
            r0 = jnp.where(lane0, 1.0, jnp.where(lane1, 0.0, r0))
            r1 = jnp.where(lane1, 1.0, jnp.where(lane0, 0.0, r1))
            n0 = (v * d) * r0 - (q * d) * r1
            n1 = (p * d) * r1 - (u * d) * r0
            rest = jnp.where(col0 | col1, 0.0, a) - c0 * n0 - c1 * n1
            out.append(jnp.where(row0, n0, jnp.where(row1, n1, rest)))
        return tuple(out)

    return lax.fori_loop(0, PROJ // 2, step, tuple(mats))


def inverse_kernel(count, factor_ref, out_ref):
    rows, cols = iota((PROJ, PROJ), 0), iota((PROJ, PROJ), 1)
    mats = []
    for n in range(2):
        factor = factor_ref[n] * (1.0 / count)
        diagonal = jnp.where(rows == cols, factor, 0.0)
        trace = jnp.sum(jnp.sum(diagonal, axis=1, keepdims=True), axis=0, keepdims=True)
        mats.append(factor + jnp.where(rows == cols, DAMPING * (trace / PROJ), 0.0))
    for n, inverse in enumerate(invert(mats)):
        out_ref[n] = inverse.astype(BF16)


def inverses(factors, count):
    return pl.pallas_call(
        lambda *refs: inverse_kernel(count, *refs),
        out_shape=jax.ShapeDtypeStruct((2, PROJ, PROJ), BF16),
        in_specs=[VMEM],
        out_specs=VMEM,
        compiler_params=pltpu.CompilerParams(vmem_limit_bytes=8 << 20),
        cost_estimate=pl.CostEstimate(flops=10**8, bytes_accessed=1 << 20, transcendentals=0),
        name="inverses",
    )(factors)


def expand(inverse_ref, wide_in_ref, wide_out_ref):
    r, i = iota((256, PROJ), 0), iota((256, PROJ), 1)
    pick_in = (i == (r // 32) * 8 + r % 8).astype(BF16)
    j, c = iota((PROJ, 256), 0), iota((PROJ, 256), 1)
    spread_in = (c % PROJ == j).astype(BF16)
    r, c = iota((256, 256), 0), iota((256, 256), 1)
    part = jnp.dot(pick_in, inverse_ref[0], preferred_element_type=F32).astype(BF16)
    part = jnp.dot(part, spread_in, preferred_element_type=F32)
    wide_in_ref[...] = jnp.where((r // 8) % 4 == c // PROJ, part, 0.0).astype(BF16)
    r, o = iota((512, PROJ), 0), iota((512, PROJ), 1)
    pick_out = (o == r // 8).astype(BF16)
    o, c = iota((PROJ, 512), 0), iota((PROJ, 512), 1)
    spread_out = (o == c // 8).astype(BF16)
    r, c = iota((512, 512), 0), iota((512, 512), 1)
    part = jnp.dot(pick_out, inverse_ref[1], preferred_element_type=F32).astype(BF16)
    part = jnp.dot(part, spread_out, preferred_element_type=F32)
    wide_out_ref[...] = jnp.where(r % 8 == c % 8, part, 0.0).astype(BF16)


def fetch_queries(near, far, use_near, query_buf, query_sem):
    copies = [
        [pltpu.make_async_copy(r, query_buf.at[n], query_sem.at[n]) for n, r in enumerate(refs)]
        for refs in (near, far)
    ]

    @pl.when(use_near)
    def _():
        start_all(copies[0])

    @pl.when(jnp.logical_not(use_near))
    def _():
        start_all(copies[1])

    return copies[0]


def condition_layer(places, me, copies, query_buf, half_ref, wide_in_ref, wide_out_ref, store):
    y, co = (me // 2) % 4, me % 2
    toward = 2 * co - 1
    width = half_ref.shape[-1]
    for n, (dy, along, dco) in enumerate(places):
        copies[n].wait()
        block = ((y + dy + along * toward + 4) % 4) * 2 + jnp.bitwise_xor(co, dco)
        for part in range(2):
            half = jnp.dot(
                wide_in_ref[...],
                query_buf[n, part * 256 : (part + 1) * 256, :],
                preferred_element_type=F32,
            ).astype(BF16)
            start = pl.multiple_of((block * 2 + part) * 32, 32)
            half_ref[:, pl.ds(start, 32), :] = half.reshape(8, 32, width)

    @pl.loop(0, 4)
    def _(k):
        both = [
            jnp.dot(wide_out_ref[...], half_ref[2 * k + g], preferred_element_type=F32)
            .reshape(PROJ, 8, width)
            for g in range(2)
        ]
        store(k, pl.multiple_of(16 * k, 16), jnp.concatenate(both, axis=1).astype(BF16))


def first_kernel(places, me_row_ref, me_col_ref, inverse_ref, *refs):
    near, far = refs[:8], refs[8:16]
    out_ref, query_buf, half_ref, wide_in_ref, wide_out_ref, query_sem = refs[16:]
    me = me_row_ref[0]
    layer = (me_col_ref[0] // 8) % 2
    copies = fetch_queries(near, far, me // 8 == layer, query_buf, query_sem)
    expand(inverse_ref, wide_in_ref, wide_out_ref)

    def store(k, start, value):
        out_ref[:, pl.ds(start, 16), :] = value

    condition_layer(places, me, copies, query_buf, half_ref, wide_in_ref, wide_out_ref, store)


def condition_first(me_row, me_col, inverse, near, far, places):
    width = near[0].shape[-1]
    return pl.pallas_call(
        lambda *refs: first_kernel(places, *refs),
        out_shape=jax.ShapeDtypeStruct((PROJ, PROJ, width), BF16),
        in_specs=[SMEM, SMEM, VMEM] + [ANY] * 16,
        out_specs=VMEM,
        scratch_shapes=[
            pltpu.VMEM((8, 512, width), BF16),
            pltpu.VMEM((8, 512, width), BF16),
            pltpu.VMEM((256, 256), BF16),
            pltpu.VMEM((512, 512), BF16),
            pltpu.SemaphoreType.DMA((8,)),
        ],
        compiler_params=pltpu.CompilerParams(vmem_limit_bytes=18 << 20),
        cost_estimate=pl.CostEstimate(flops=3 * 10**9, bytes_accessed=8 << 20, transcendentals=0),
        name="condition_first",
    )(me_row, me_col, inverse, *near, *far)


def input_kernel(x_ref, out_ref):
    x = x_ref[...]
    gram = lax.dot_general(x, x, (((0,), (0,)), ((), ())), preferred_element_type=F32)
    gram = jnp.where(iota(gram.shape, 0) // PROJ == iota(gram.shape, 1) // PROJ, gram, 0.0)
    rows = jnp.sum(gram.reshape(8, PROJ, 512), axis=0)
    fold = rows[:, :128] + rows[:, 128:256] + rows[:, 256:384] + rows[:, 384:]
    out_ref[...] = fold[:, :PROJ] + fold[:, PROJ:]


def input_factor(train):
    return pl.pallas_call(
        input_kernel,
        out_shape=jax.ShapeDtypeStruct((PROJ, PROJ), F32),
        in_specs=[VMEM],
        out_specs=VMEM,
        compiler_params=pltpu.CompilerParams(vmem_limit_bytes=8 << 20),
        cost_estimate=pl.CostEstimate(flops=3 * 10**8, bytes_accessed=1 << 20, transcendentals=0),
        name="input_factor",
    )(train)


def terms_kernel(x_ref, input_ref, out_ref, side_ref, sum_ref):
    blocks, count, _ = x_ref.shape
    for b in range(blocks):
        turned = x_ref[b].astype(F32).T.astype(BF16).reshape(8, 4, 16, count)
        parts = [turned[:, g].reshape(128, count) for g in range(4)]
        side_ref[b * 128 : (b + 1) * 128, :] = jnp.concatenate(parts, axis=1)
    for b in range(blocks):
        gram = lax.dot_general(
            side_ref[b * 128 : (b + 1) * 128, :],
            side_ref[...],
            (((1,), (1,)), ((), ())),
            preferred_element_type=F32,
        )
        gram = jnp.where(iota(gram.shape, 0) % 16 == iota(gram.shape, 1) % 16, gram, 0.0)
        sum_ref[8 * b : 8 * b + 8, :] = jnp.sum(gram.reshape(8, 16, 1024), axis=1)
    ones = (iota((1024, PROJ), 0) // 16 == iota((1024, PROJ), 1)).astype(BF16)
    rest = sum_ref[...]
    total = jnp.zeros((PROJ, PROJ), F32)
    for _ in range(3):
        part = rest.astype(BF16)
        total += jnp.dot(part, ones, preferred_element_type=F32)
        rest = rest - part.astype(F32)
    out_ref[0] = input_ref[...]
    out_ref[1] = total


def factor_terms(blocks, input_term):
    count = blocks.shape[1]
    return pl.pallas_call(
        terms_kernel,
        out_shape=jax.ShapeDtypeStruct((2, PROJ, PROJ), F32),
        in_specs=[VMEM, VMEM],
        out_specs=VMEM,
        scratch_shapes=[pltpu.VMEM((1024, 4 * count), BF16), pltpu.VMEM((PROJ, 1024), F32)],
        compiler_params=pltpu.CompilerParams(vmem_limit_bytes=12 << 20),
        cost_estimate=pl.CostEstimate(flops=6 * 10**8, bytes_accessed=1 << 20, transcendentals=0),
        name="factor_terms",
    )(blocks, input_term)


def column_of(me, k, other):
    toward = jnp.where((me // 16) % 2 == 0, -k, k)
    return ((me // 2 + toward) % 8) * 2 + jnp.bitwise_xor(me % 2, other)


def start_all(copies):
    for copy in copies:
        copy.start()
    return copies


def main_kernel(places, own_places, me_row_ref, me_col_ref, inverse_ref, first_ref, *refs):
    near, far, theirs_refs, refs = refs[:8], refs[8:16], refs[16:22], refs[22:]
    own_refs, refs = refs[: len(own_places)], refs[len(own_places) :]
    out_ref, own_ref, late_ref, query_buf, half_ref, cond_ref, sum_ref, wide_in_ref, wide_out_ref = refs[:9]
    theirs_buf, own_buf, query_sem, theirs_sem, own_sem, late_sem, first_sem = refs[9:]

    me = me_row_ref[0]
    layer = (me_col_ref[0] // 8) % 2
    query_copies = fetch_queries(near, far, me // 8 != layer, query_buf, query_sem)
    first_start = pl.multiple_of(layer * PROJ, PROJ)
    first_copy = pltpu.make_async_copy(first_ref, cond_ref.at[pl.ds(first_start, PROJ)], first_sem.at[0])
    first_copy.start()
    theirs_copies = start_all(
        [pltpu.make_async_copy(r, theirs_buf.at[n], theirs_sem.at[n]) for n, r in enumerate(theirs_refs)]
    )
    own_copies = start_all(
        [
            pltpu.make_async_copy(r, own_buf.at[pl.ds(first * 512, slots * 512)], own_sem.at[first])
            for r, (first, slots) in zip(own_refs, own_places)
        ]
    )
    expand(inverse_ref, wide_in_ref, wide_out_ref)
    width = half_ref.shape[-1]
    second_start = pl.multiple_of((1 - layer) * PROJ, PROJ)

    def store(k, start, value):
        cond_ref[pl.ds(second_start, PROJ), pl.ds(start, 16), :] = value

    condition_layer(places, me, query_copies, query_buf, half_ref, wide_in_ref, wide_out_ref, store)
    first_copy.wait()

    me = me_col_ref[0]
    late_copies = start_all(
        [
            pltpu.make_async_copy(
                cond_ref.at[pl.ds(column_of(me, 3 + n // 2, n % 2) * 8, 8)], late_ref.at[n], late_sem.at[n]
            )
            for n in range(4)
        ]
    )

    def cond_of(k, other):
        return cond_ref[pl.ds(column_of(me, k, other) * 8, 8)].reshape(512, width)

    for n in range(6):
        theirs_copies[n].wait()
        part = jnp.dot(theirs_buf[n], cond_of(1 + n // 2, n % 2), preferred_element_type=F32)
        sum_ref[...] = part if n == 0 else sum_ref[...] + part
    out_ref[...] = sum_ref[...].astype(BF16)
    waits = {first: copy for copy, (first, _) in zip(own_copies, own_places)}
    for n in range(6):
        if n in waits:
            waits[n].wait()
        part = jnp.dot(
            own_buf[n * 512 : (n + 1) * 512, :], cond_of(n // 2, n % 2), preferred_element_type=F32
        )
        own_ref[...] = part if n == 0 else own_ref[...] + part
    for copy in late_copies:
        copy.wait()


def condition_and_score(me_row, me_col, inverse, first, near, far, places, theirs, own, own_places):
    width = near[0].shape[-1]
    return pl.pallas_call(
        lambda *refs: main_kernel(places, own_places, *refs),
        out_shape=(
            jax.ShapeDtypeStruct((512, width), BF16),
            jax.ShapeDtypeStruct((512, width), F32),
            jax.ShapeDtypeStruct((4, 8, PROJ, width), BF16),
        ),
        in_specs=[SMEM, SMEM, VMEM, ANY] + [ANY] * (16 + len(theirs) + len(own)),
        out_specs=(VMEM, VMEM, HBM),
        scratch_shapes=[
            pltpu.VMEM((8, 512, width), BF16),
            pltpu.VMEM((8, 512, width), BF16),
            pltpu.VMEM((LAYERS * PROJ, PROJ, width), BF16),
            pltpu.VMEM((512, width), F32),
            pltpu.VMEM((256, 256), BF16),
            pltpu.VMEM((512, 512), BF16),
            pltpu.VMEM((6, 512, 512), BF16),
            pltpu.VMEM((6 * 512, 512), BF16),
            pltpu.SemaphoreType.DMA((8,)),
            pltpu.SemaphoreType.DMA((6,)),
            pltpu.SemaphoreType.DMA((6,)),
            pltpu.SemaphoreType.DMA((4,)),
            pltpu.SemaphoreType.DMA((1,)),
        ],
        compiler_params=pltpu.CompilerParams(vmem_limit_bytes=28 << 20),
        cost_estimate=pl.CostEstimate(flops=6 * 10**9, bytes_accessed=18 << 20, transcendentals=0),
        name="condition_and_score",
    )(me_row, me_col, inverse, first, *near, *far, *theirs, *own)


def own_kernel(total_ref, cond_ref, near_ref, far_ref, out_ref):
    total = total_ref[...]
    for n in range(4):
        ref = (near_ref, far_ref)[n // 2]
        rows = ref[n % 2 * 512 : (n % 2 + 1) * 512, :]
        total += jnp.dot(
            rows, cond_ref[n].reshape(512, cond_ref.shape[-1]), preferred_element_type=F32
        )
    out_ref[...] = total


def score_own(total, cond, near, far):
    return pl.pallas_call(
        own_kernel,
        out_shape=jax.ShapeDtypeStruct(total.shape, F32),
        in_specs=[VMEM] * 4,
        out_specs=VMEM,
        compiler_params=pltpu.CompilerParams(vmem_limit_bytes=12 << 20),
        cost_estimate=pl.CostEstimate(flops=10**9, bytes_accessed=5 << 20, transcendentals=0),
        name="score_own",
    )(total, cond, near, far)


def all_of(value, axis, size):
    total = value
    for k in range(1, size):
        total = total + lax.ppermute(value, axis, [(i, i ^ k) for i in range(size)])
    return total


def local(train, query):
    rows = train.shape[0]
    features = train.shape[1] * 16
    partner = swap(train, "xl")
    ex = lax.all_to_all(train.reshape(8, rows // 8, 512), ("zl", "xl"), 0, 0, tiled=True)
    total = factor_terms(ex, input_factor(train))
    total = all_of(total, "co", 2)
    total = all_of(total, "y", 4)
    total = all_of(total, ("xh", "xl"), 4)
    total = all_of(total, "zl", 4)
    inverse = inverses(total, rows * 16 * PROJ)
    other_inverse = swap(inverse, "zh")

    queries = []
    for tag in "qx":
        value = query.T if tag == "q" else swap(value, "xh")
        other = swap(value, "co")
        next_own = ring(value, ("y", "co"), 4)
        next_other = ring(other, ("y", "co"), 4)
        far_own = ring(next_own, ("y", "co"), 4)
        queries.append(
            [
                value,
                other,
                next_own,
                next_other,
                swap(next_own, "co"),
                swap(next_other, "co"),
                far_own,
                swap(far_own, "co"),
            ]
        )
    places = ((0, 0, 0), (0, 0, 1), (0, 1, 0), (0, 1, 1), (0, -1, 1), (0, -1, 0), (2, 0, 0), (2, 0, 1))

    a = jnp.concatenate([train, partner], axis=0)
    b = swap(train, "co")
    ring_axes = ("co",) + Z
    mine, others = [train, partner], []
    for k in range(1, 5):
        a = ring(a, ring_axes, 8)
        mine.append(a)
        if k < 4:
            b = ring(b, ring_axes, 8)
            others += [b, swap(b, "xl")]
    me_row = lax.axis_index(ROW).astype(jnp.int32).reshape(1)
    me_col = lax.axis_index(("co",) + COL).astype(jnp.int32).reshape(1)
    own_places = ((0, 1), (1, 1), (2, 2), (4, 2))
    first = condition_first(me_row, me_col, inverse, *queries, places)
    theirs, own, cond = condition_and_score(
        me_row, me_col, other_inverse, first, *queries, places, others, mine[:4], own_places
    )
    theirs = swap(theirs, "co").astype(F32)
    return (score_own(own, cond, *mine[4:]) + theirs) * (1.0 / math.sqrt(features))


def solution(mesh):
    torus = Mesh(mesh.devices.reshape(2, 4, 2, 2, 4, 2), ROW + COL)
    in_specs = (P(ROW, COL), P(COL, ROW))
    return jax.shard_map(local, mesh=torus, in_specs=in_specs, out_specs=P(ROW, COL), check_vma=False)
```
